32 devices in a mesh: grp: 2 (over x), gx: 8 (over z, y), gy: 2 (over core).
Axes of the slice: x: 2, y: 2, z: 4, core: 2. Of those that a mesh axis runs over, the one named last changes fastest.
Arguments:
- ice_blocks: int32 [2048], replicated, may hold values from 0 to 4095, as said below
- ice_conc: float32 [2048, 5, 256], P(('grp', 'gx', 'gy')), may hold values from 0.02 to 0.19
- ice_thick: float32 [2048, 5, 256], P(('grp', 'gx', 'gy')), may hold values from 0.1 to 5
- ice_snow: float32 [2048, 5, 256], P(('grp', 'gx', 'gy')), may hold values from 0.01 to 0.5
- ice_temp: float32 [2048, 5, 7, 256], P(('grp', 'gx', 'gy')), may hold values from -6 to 6
- sw_down: float32 [2048, 3, 256], P(('grp', 'gx', 'gy')), may hold values from 0.2 to 2
- ocean_temp: float32 [8, 2048, 512], P(None, 'gx', ('grp', 'gy')), may hold values from -6 to 6
- ocean_salt: float32 [8, 2048, 512], P(None, 'gx', ('grp', 'gy')), may hold values from -6 to 6
- ocean_east: float32 [2048, 512], P('gx', ('grp', 'gy')), may hold values from -6 to 6
- ocean_north: float32 [2048, 512], P('gx', ('grp', 'gy')), may hold values from -6 to 6
- land_mask: int32 [2048, 512], P('gx', ('grp', 'gy')), may hold values 0 or 1
Outputs:
- ice_temp_out: float32 [2048, 5, 7, 256], P(('grp', 'gx', 'gy'))
- ice_thick_out: float32 [2048, 5, 256], P(('grp', 'gx', 'gy'))
- ocean_temp_out: float32 [8, 2048, 512], P(None, 'gx', ('grp', 'gy'))
- ocean_salt_out: float32 [8, 2048, 512], P(None, 'gx', ('grp', 'gy'))
The draws below stay inside these ranges and needn't reach their ends.
Inputs may be any that keep to these rules, and one draw needn't show every extreme that they name: `ice_blocks`: all entries differ. Entry g is held by device g // 64 (devices ordered grp, gx, gy, slowest first). The ocean tile of device (p, q, r) holds blocks with b // 32 // 16 == q and b % 32 // 8 == p * 2 + r. The blocks that one device holds in one device's tile number at most 4, exactly 4 for some pairs; a tile holds at most 128 of them, and some tile all 128.
All inputs are finite; a program needn't handle non-finite values. No bound on the sum of `land_mask` on one device may be relied on, other than what follows from the above.
Results may differ from the reference program's by a relative error of at most 0.0001.
Values sent between devices are 32-bit elements; how exact they have to be, the bound alone decides.
No kernel may reach another device: no remote copies, remote signals or barrier semaphores. Data moves between devices by JAX's collectives and lax.ppermute only.
A program may use at most 128 MiB of HBM per device.

```python
import math
import jax
import jax.numpy as jnp
from jax import lax

BSIDE = 16
TXB = 16
TYB = 8
CATS = 5
LAYERS = 7
BANDS = 3
LEVELS = 8
NSTEP = 4
NB_DEV = 64
NB = 2048
BC = 256
NBX = 128
NBY = 32
NX = 2048
NY = 512
N_GX = 8
N_GY = 2
DEVICES = 32


def draw_ice_blocks(key, part):
    tiles = DEVICES
    per_tile = TXB * TYB
    key_order = jax.random.fold_in(key, 11)
    key_pick = jax.random.fold_in(key, 23)
    order = jax.random.permutation(key_order, tiles)
    position = jnp.argsort(order).astype(jnp.int32)
    count = jnp.where(position < tiles // 4, per_tile, jnp.where(position < 3 * tiles // 4, per_tile // 2, 0))
    scores = jax.random.randint(key_pick, (tiles, per_tile), 0, 1 << 20) * per_tile + jnp.arange(per_tile, dtype=jnp.int32)[None, :]
    ranks = jnp.argsort(jnp.argsort(scores, axis=1), axis=1).astype(jnp.int32)
    chosen = ranks < count[:, None]
    codes = jnp.arange(tiles, dtype=jnp.int32)[:, None] * per_tile + jnp.arange(per_tile, dtype=jnp.int32)[None, :]
    codes = jnp.where(chosen, codes, tiles * per_tile).reshape(-1)
    listed = jnp.sort(codes)[:NB]
    tile_index = listed // per_tile
    local = listed % per_tile
    plane = N_GX * N_GY
    tile_x = tile_index % plane // N_GY
    tile_y = tile_index // plane * N_GY + tile_index % N_GY
    block_x = tile_x * TXB + local // TYB
    block_y = tile_y * TYB + local % TYB
    ident = block_x * NBY + block_y
    slots = jnp.arange(NB, dtype=jnp.int32)
    holder = slots // NB_DEV
    within = slots % NB_DEV
    curve = 2 * (within // 2 * DEVICES + holder) + within % 2
    return jnp.take(ident, curve).astype(jnp.int32)


def set_ends(drawn, rng, smallest, high):
    place = [jax.random.randint(jax.random.fold_in(rng, axis), (), 0, length) for axis, length in enumerate(drawn.shape)]
    main_axis = drawn.shape.index(max(drawn.shape))
    next_to = place[:main_axis] + [(place[main_axis] + 1) % drawn.shape[main_axis]] + place[main_axis + 1:]
    return drawn.at[tuple(place)].set(smallest).at[tuple(next_to)].set(high)


def block_levels(stream_key, extent, pieces, smallest, top_value):
    def one(dim, blocks):
        heights = jax.random.uniform(jax.random.fold_in(jax.random.fold_in(stream_key, 6), dim), (blocks,), jnp.float32, smallest / len(pieces), top_value / len(pieces))
        return jnp.repeat(jnp.exp(heights), extent[dim] // blocks).reshape((-1,) + (1,) * (len(extent) - dim - 1))

    loudness = one(*pieces[0])
    for cut in pieces[1:]:
        loudness = loudness * one(*cut)
    return loudness


def noise(key, extent, spread, bound, cuts=(), kind=jnp.bfloat16):
    entries = spread * jax.random.normal(key, extent, jnp.float32)
    if cuts:
        entries = entries * block_levels(key, extent, cuts, -0.22, 0.18)
    return jnp.clip(entries, -bound, bound).astype(kind)


def setup_inputs(seed: int = 0) -> dict:
    keys = jax.random.split(jax.random.key(seed), 12)
    ice_blocks = draw_ice_blocks(jax.random.fold_in(keys[11], 71), 0)
    ice_conc = jnp.clip(0.02 + 0.17 * jax.random.uniform(keys[1], (NB, CATS, BC), jnp.float32) ** block_levels(keys[1], (NB, CATS, BC), ((0, 32),), -0.2, 0.2), 0.02, 0.19)
    ice_thick = jnp.clip(jnp.exp(math.log(5.0) - 3.912023 * jax.random.uniform(keys[2], (NB, CATS, BC), jnp.float32) ** block_levels(keys[2], (NB, CATS, BC), ((0, 32),), -0.2, 0.2)), 0.1, 5.0)
    ice_snow = jnp.clip(jnp.exp(math.log(0.5) - 3.912023 * jax.random.uniform(keys[3], (NB, CATS, BC), jnp.float32) ** block_levels(keys[3], (NB, CATS, BC), ((0, 32),), -0.2, 0.2)), 0.01, 0.5)
    ice_temp = noise(keys[4], (NB, CATS, LAYERS, BC), 1.0, 6.0, ((0, 32),), jnp.float32)
    sw_down = jnp.clip(jnp.exp(math.log(2.0) - 2.3025851 * jax.random.uniform(keys[5], (NB, BANDS, BC), jnp.float32) ** block_levels(keys[5], (NB, BANDS, BC), ((0, 32),), -0.2, 0.2)), 0.2, 2.0)
    ocean_temp = noise(keys[6], (LEVELS, NX, NY), 1.0, 6.0, ((1, 8), (2, 4)), jnp.float32)
    ocean_salt = noise(keys[7], (LEVELS, NX, NY), 1.0, 6.0, ((1, 8), (2, 4)), jnp.float32)
    ocean_east = noise(keys[8], (NX, NY), 1.0, 6.0, ((0, 8), (1, 4)), jnp.float32)
    ocean_north = noise(keys[9], (NX, NY), 1.0, 6.0, ((0, 8), (1, 4)), jnp.float32)
    land_mask = set_ends((jax.random.randint(keys[10], (NX, NY), 0, 10) < 9).astype(jnp.int32), jax.random.fold_in(keys[10], 1), 0, 1)
    return dict(ice_blocks=ice_blocks, ice_conc=ice_conc, ice_thick=ice_thick, ice_snow=ice_snow, ice_temp=ice_temp, sw_down=sw_down, ocean_temp=ocean_temp, ocean_salt=ocean_salt, ocean_east=ocean_east, ocean_north=ocean_north, land_mask=land_mask)


ALBEDO_ICE = (0.78, 0.64, 0.45)
SNOW_EXT = (2.0, 5.0, 10.0)
ICE_EXT = (0.8, 2.0, 6.0)
DEPTH_SCALE = (1.0, 8.0, 25.0)
LEVEL_DEPTH = 10.0
KAPPA = 0.2

def ice_optics(conc, thick, snow, sw_rays, layers):
    bare = jnp.exp(-thick / 0.5)
    open_frac = 1.0 - lax.optimization_barrier(jnp.sum(conc, axis=1))
    surface = jnp.zeros_like(thick)
    heating = [jnp.zeros_like(thick) for layer_index in range(layers)]
    passed = []
    for band_index in range(3):
        down = sw_rays[:, band_index][:, None, :]
        albedo = ALBEDO_ICE[band_index] * (1.0 - bare) + 0.06 * bare
        top_flux = down * (1.0 - albedo)
        current = top_flux * jnp.exp(-SNOW_EXT[band_index] * snow)
        surface = surface + (top_flux - current)
        factor = jnp.exp(-ICE_EXT[band_index] * thick / layers)
        for layer_index in range(layers):
            after = current * factor
            heating[layer_index] = heating[layer_index] + (current - after)
            current = after
        passed.append(lax.optimization_barrier(jnp.sum(conc * current, axis=1)) + open_frac * sw_rays[:, band_index] * 0.94)
    return (jnp.stack(heating, axis=2), passed, surface)

def ice_fluxes(conc, thick, snow, sw_rays, temps):
    layers = temps.shape[2]
    heating, passed, surface = ice_optics(conc, thick, snow, sw_rays, layers)
    heat_ice = lax.optimization_barrier(jnp.sum(conc * 0.05 * temps[:, :, layers - 1] * layers / thick, axis=1))
    fresh = lax.optimization_barrier(jnp.sum(conc * snow * surface, axis=1))
    return (jnp.stack(passed + [heat_ice, fresh], axis=1), heating)

def ice_update(thick, temps, heating, returned):
    layers = temps.shape[2]
    sea_temp = returned[:, 0]
    sea_salt = returned[:, 1]
    east_vel = returned[:, 2]
    north_vel = returned[:, 3]
    freezing = -0.3 * sea_salt
    stress = jnp.sqrt(east_vel * east_vel + north_vel * north_vel + 1.0)
    thick_new = thick * jnp.exp(-0.1 * stress * (sea_temp - freezing))[:, None, :]
    warmed = temps + 0.1 * heating * layers / thick[:, :, None, :]
    bottom = warmed[:, :, layers - 1:] + 0.3 * (freezing[:, None, None, :] - temps[:, :, layers - 1:])
    return (jnp.concatenate([warmed[:, :, :layers - 1], bottom], axis=2), thick_new)

def tracer_step(state):
    fields = state[:-1]
    wet = state[-1:]
    centre = fields[:, 1:-1, 1:-1]
    wet_c = wet[:, 1:-1, 1:-1]
    total = jnp.zeros_like(centre)
    pairs = ((fields[:, 2:, 1:-1], wet[:, 2:, 1:-1]), (fields[:, :-2, 1:-1], wet[:, :-2, 1:-1]), (fields[:, 1:-1, 2:], wet[:, 1:-1, 2:]), (fields[:, 1:-1, :-2], wet[:, 1:-1, :-2]))
    for values, wet_n in pairs:
        total = total + wet_n * (values - centre)
    return jnp.concatenate([centre + KAPPA * wet_c * total, wet_c], axis=0)

def absorb(temp, salt, forcing, wet):
    levels = temp.shape[0]
    rows = []
    for level_index in range(levels):
        upper = LEVEL_DEPTH * level_index
        lower = LEVEL_DEPTH * (level_index + 1)
        gain = jnp.zeros_like(wet)
        for band_index in range(3):
            share = math.exp(-upper / DEPTH_SCALE[band_index])
            if level_index < levels - 1:
                share = share - math.exp(-lower / DEPTH_SCALE[band_index])
            gain = gain + share * forcing[band_index]
        if level_index == 0:
            gain = gain + forcing[3]
        rows.append(temp[level_index] + 0.5 * wet * gain)
    salt_top = salt[0] - 0.5 * wet * forcing[4]
    return (jnp.stack(rows), jnp.concatenate([salt_top[None], salt[1:]], axis=0))

def extend_global(state):
    wide = jnp.concatenate([state[:, -1:, :], state, state[:, :1, :]], axis=1)
    south = jnp.zeros_like(wide[:, :, :1])
    north = wide[:, ::-1, -1:]
    return jnp.concatenate([south, wide, north], axis=2)

def reference(ice_blocks, ice_conc, ice_thick, ice_snow, ice_temp, sw_down, ocean_temp, ocean_salt, ocean_east, ocean_north, land_mask):
    payload, heating = ice_fluxes(ice_conc, ice_thick, ice_snow, sw_down, ice_temp)
    cells = BSIDE * BSIDE
    total_blocks = NBX * NBY
    grid_blocks = jnp.zeros((total_blocks, 5, cells), jnp.float32).at[ice_blocks].set(payload)
    forcing = grid_blocks.reshape(NBX, NBY, 5, BSIDE, BSIDE).transpose(2, 0, 3, 1, 4).reshape(5, NX, NY)
    wet = land_mask.astype(jnp.float32)
    diffused = []
    for tracer in (ocean_temp, ocean_salt):
        state = jnp.concatenate([tracer, wet[None]], axis=0)
        for step_index in range(NSTEP):
            state = tracer_step(extend_global(state))
        diffused.append(state[:-1])
    temp_new, salt_new = absorb(diffused[0], diffused[1], forcing, wet)
    surface = jnp.stack([temp_new[0], salt_new[0], ocean_east, ocean_north])
    returned = surface.reshape(4, NBX, BSIDE, NBY, BSIDE).transpose(1, 3, 0, 2, 4).reshape(total_blocks, 4, cells)
    returned = jnp.take(returned, ice_blocks, axis=0)
    temps_new, thick_new = ice_update(ice_thick, ice_temp, heating, returned)
    return (temps_new, thick_new, temp_new, salt_new)
```

```python
import functools
import math

import jax
import jax.numpy as jnp
from jax import lax
from jax.experimental import pallas as pl
from jax.experimental.pallas import tpu as pltpu
from jax.sharding import PartitionSpec as P

NSTEP = 4
ALBEDO_ICE = (0.78, 0.64, 0.45)
SNOW_EXT = (2.0, 5.0, 10.0)
ICE_EXT = (0.8, 2.0, 6.0)
DEPTH_SCALE = (1.0, 8.0, 25.0)
LEVEL_DEPTH = 10.0
KAPPA = 0.2
LANES = 128
SUB = 8
BASE = 16

AXES = ("grp", "gx", "gy")
VMEM = pl.BlockSpec(memory_space=pltpu.VMEM)
SMEM = pl.BlockSpec(memory_space=pltpu.SMEM)
F32 = jnp.float32


def quot(x, n):
    return x >> (n.bit_length() - 1) if n & (n - 1) == 0 else x // n


def rest(x, n):
    return x & (n - 1) if n & (n - 1) == 0 else x % n


def iota(shape, dim):
    return lax.broadcasted_iota(jnp.int32, shape, dim)


def swap_chunks(x, side):
    rows = x.shape[0]
    x = x.reshape(rows // SUB, SUB, LANES)
    row = iota(x.shape, 1)
    chunk = quot(iota(x.shape, 2), side)
    for bit in range(3):
        step = 1 << bit
        r = (row >> bit) & 1
        c = (chunk >> bit) & 1
        down = pltpu.roll(pltpu.roll(x, step, 1), LANES - side * step, 2)
        up = pltpu.roll(pltpu.roll(x, SUB - step, 1), side * step, 2)
        x = jnp.where(r == c, x, jnp.where(r == 1, down, up))
    return x.reshape(rows, LANES)


def table_kernel(dims, me_ref, blocks_ref, tab_ref):
    n_gx, n_gy, n_rows, blocks_x, blocks_y, per_dev, cap, devices = dims
    me = me_ref[0]
    rows = blocks_ref.shape[0]
    per_tile = blocks_x * blocks_y
    slots = devices * cap

    def place(blocks):
        column = quot(blocks, blocks_y * n_rows)
        row_pos = rest(blocks, blocks_y * n_rows)
        owner_x = quot(column, blocks_x)
        owner_y = quot(row_pos, blocks_y)
        owner = quot(owner_y, n_gy) * (n_gx * n_gy) + owner_x * n_gy + rest(owner_y, n_gy)
        return owner, rest(column, blocks_x) * blocks_y + rest(row_pos, blocks_y)

    owner, local = place(blocks_ref[...])
    mine = owner == me
    i = iota((LANES, LANES), 0)
    j = iota((LANES, LANES), 1)
    before = (i < j) & (quot(i, per_dev) == quot(j, per_dev))
    rank = jnp.dot(
        mine.astype(F32), before.astype(F32), preferred_element_type=F32
    ).astype(jnp.int32)
    holder = quot(iota(owner.shape, 0) * LANES + iota(owner.shape, 1), per_dev)
    recv = holder * cap + rank
    by_local = jnp.where(mine, local, -1)
    by_recv = jnp.where(mine, recv, -1)
    source = jnp.zeros((per_tile, LANES), F32)
    block = jnp.zeros((slots, LANES), F32)
    tile_iota = iota((per_tile, LANES), 0)
    slot_iota = iota((slots, LANES), 0)
    for r in range(rows):
        hit = tile_iota == by_local[r : r + 1, :]
        source = source + jnp.where(hit, (recv[r : r + 1, :] + 1).astype(F32), 0.0)
        hit = slot_iota == by_recv[r : r + 1, :]
        block = block + jnp.where(hit, local[r : r + 1, :].astype(F32), 0.0)
    tab_ref[1:2, :] = (jnp.sum(source.T, axis=0, keepdims=True) - 1.0).astype(jnp.int32)
    block_row = jnp.sum(block.T, axis=0, keepdims=True).astype(jnp.int32)
    for k in range(slots // LANES):
        tab_ref[2 + k : 3 + k, :] = block_row[:, k * LANES : (k + 1) * LANES]

    start = me * per_dev
    own, _ = place(blocks_ref[pl.ds(quot(start, LANES), 1), :])
    wide = jnp.broadcast_to(own.astype(F32), (LANES, LANES))
    same = (wide == wide.T) & before
    rank = jnp.sum(same.astype(F32), axis=0, keepdims=True).astype(jnp.int32)
    slot = own * cap + rank
    slot = pltpu.roll(
        jnp.broadcast_to(slot, (SUB, LANES)), rest(LANES - rest(start, LANES), LANES), 1
    )
    tab_ref[0:1, :] = slot[0:1, :]


def optics_kernel(cap, tab_ref, conc_ref, thick_ref, snow_ref, sw_ref, last_ref, send_ref, pay):
    cats, chunk, cells = conc_ref.shape
    halves = cells // LANES
    fields = 5 * halves
    layers = 7
    open_frac = 1.0
    heat = 0.0
    fresh = 0.0
    passed = [0.0, 0.0, 0.0]
    downs = [sw_ref[b] for b in range(3)]
    for c in range(cats):
        conc = conc_ref[c]
        thick = thick_ref[c]
        snow = snow_ref[c]
        bare = jnp.exp(-thick / 0.5)
        thin = jnp.exp(-ICE_EXT[0] * thick)
        light = jnp.exp(-SNOW_EXT[0] * snow)
        middle = jnp.exp(-SNOW_EXT[1] * snow)
        through_snow = (light, middle, middle * middle)
        through_ice = (thin, bare, bare * bare * bare)
        surface = 0.0
        for b in range(3):
            albedo = ALBEDO_ICE[b] * (1.0 - bare) + 0.06 * bare
            top = downs[b] * (1.0 - albedo)
            current = top * through_snow[b]
            surface = surface + (top - current)
            passed[b] = passed[b] + conc * (current * through_ice[b])
        open_frac = open_frac - conc
        heat = heat + conc * 0.05 * last_ref[c, 0] * layers / thick
        fresh = fresh + conc * snow * surface
    values = [passed[b] + open_frac * downs[b] * 0.94 for b in range(3)] + [heat, fresh]
    for f in range(5):
        for h in range(halves):
            k = f * halves + h
            pay[k * chunk : (k + 1) * chunk, :] = values[f][:, h * LANES : (h + 1) * LANES]
    first = pl.program_id(0) * chunk
    for i in range(chunk):
        slot = tab_ref[0, first + i]
        send_ref[quot(slot, cap), pl.ds(rest(slot, cap) * fields, fields), :] = pay[
            pl.ds(i, fields, stride=chunk), :
        ]


def warm_kernel(thick_ref, snow_ref, sw_ref, temp_ref, warm_ref):
    layers = temp_ref.shape[1]
    downs = [sw_ref[b] for b in range(3)]
    thick = thick_ref[0]
    snow = snow_ref[0]
    bare = jnp.exp(-thick / 0.5)
    light = jnp.exp(-SNOW_EXT[0] * snow)
    middle = jnp.exp(-SNOW_EXT[1] * snow)
    through_snow = (light, middle, middle * middle)
    scale = 0.1 * layers / thick
    currents = []
    factors = []
    for b in range(3):
        albedo = ALBEDO_ICE[b] * (1.0 - bare) + 0.06 * bare
        currents.append(downs[b] * (1.0 - albedo) * through_snow[b])
        factors.append(jnp.exp(-ICE_EXT[b] * thick / layers))
    for l in range(layers):
        heating = 0.0
        for b in range(3):
            after = currents[b] * factors[b]
            heating = heating + (currents[b] - after)
            currents[b] = after
        old = temp_ref[0, l]
        new = old + heating * scale
        if l == layers - 1:
            new = new - 0.3 * old
        warm_ref[0, l] = new


def finish_kernel(cap, tab_ref, ans_ref, thick_ref, warm_ref, thick_out, temp_out, got):
    cats, per_dev, cells = thick_ref.shape
    halves = cells // LANES
    fields = 2 * halves
    for i in range(per_dev):
        slot = tab_ref[0, i]
        got[pl.ds(i, fields, stride=per_dev), :] = ans_ref[
            quot(slot, cap), pl.ds(rest(slot, cap) * fields, fields), :
        ]
    for h in range(halves):
        lanes = slice(h * LANES, (h + 1) * LANES)
        growth = jnp.exp(got[h * per_dev : (h + 1) * per_dev, :])
        freezing = 0.3 * got[(halves + h) * per_dev : (halves + h + 1) * per_dev, :]
        for c in range(cats):
            thick_out[c, :, lanes] = thick_ref[c, :, lanes] * growth
            temp_out[c, 0, :, lanes] = warm_ref[c, 0, :, lanes] + freezing


def edge_kernel(temp_ref, salt_ref, land_ref, mix_ref, wets_ref, up_ref, down_ref, head_ref, foot_ref):
    levels, tile_x, _ = temp_ref.shape
    width = NSTEP
    chunk = 32
    fields = 2 * levels
    for r in range(0, tile_x, chunk):
        rows = slice(r, r + chunk)
        lane = iota((chunk, LANES), 1)
        group = lane >> 3
        low = (lane & 7) < width
        mix = jnp.zeros((chunk, LANES), F32)
        for f in range(fields):
            tile = temp_ref[f, rows] if f < levels else salt_ref[f - levels, rows]
            mix = jnp.where(group == f, pltpu.roll(tile, (8 * f + width) % LANES, 1), mix)
        wet = land_ref[rows].astype(F32)
        wets = jnp.where(group == 0, pltpu.roll(wet, width, 1), 0.0)
        for step in (8, 16, 32, 64):
            wets = wets + pltpu.roll(wets, step, 1)
        mix_ref[rows] = mix
        wets_ref[rows] = wets
        up_ref[rows] = jnp.where(low, mix, pltpu.roll(wets, width, 1))
        down_ref[rows] = jnp.where(low, pltpu.roll(wets, LANES - width, 1), mix)
    for f in range(fields + 1):
        to = slice(f * width, (f + 1) * width)
        for ref, at in ((head_ref, 0), (foot_ref, tile_x - width)):
            if f < levels:
                ref[to] = temp_ref[f, at : at + width]
            elif f < fields:
                ref[to] = salt_ref[f - levels, at : at + width]
            else:
                ref[to] = land_ref[at : at + width].astype(F32)


def strip_kernel(
    dims, me_ref, mix_ref, wets_ref, above_ref, below_ref, fold_ref, head_ref, foot_ref,
    left_ref, right_ref, wleft_ref, wright_ref, first_ref, last_ref,
):
    n_grp, n_gx, n_gy = dims
    me = me_ref[0]
    is_top = (quot(me, n_gx * n_gy) == n_grp - 1) & (rest(me, n_gy) == n_gy - 1)
    tile_x = mix_ref.shape[0]
    width = NSTEP
    own = head_ref.shape[0]
    lane = iota((SUB, LANES), 1)
    row = iota((SUB, LANES), 0)
    low = (lane & 7) < width
    for r in range(0, tile_x, SUB):
        rows = slice(r, r + SUB)
        mirror = fold_ref[tile_x - r - SUB : tile_x - r]
        for bit in range(3):
            step = 1 << bit
            mirror = jnp.where(
                (row >> bit) & 1 == 0,
                pltpu.roll(mirror, SUB - step, 0),
                pltpu.roll(mirror, step, 0),
            )
            mirror = jnp.where(
                (lane >> bit) & 1 == 0,
                pltpu.roll(mirror, LANES - step, 1),
                pltpu.roll(mirror, step, 1),
            )
        above = jnp.where(is_top, mirror, above_ref[rows])
        below = below_ref[rows]
        mix = mix_ref[rows]
        wets = wets_ref[rows]
        left_ref[rows] = jnp.where(low, below, mix)
        right_ref[rows] = jnp.where(low, mix, above)
        wleft_ref[rows] = jnp.where(low, pltpu.roll(below, LANES - width, 1), wets)
        wright_ref[rows] = jnp.where(low, wets, pltpu.roll(above, width, 1))
    for out, src, at in ((first_ref, head_ref, 0), (last_ref, foot_ref, tile_x - width)):
        out[0:own] = src[...]
        for k, ref in enumerate((left_ref, right_ref, wleft_ref, wright_ref)):
            out[own + k * width : own + (k + 1) * width] = ref[at : at + width]


def diffuse_kernel(
    temp_ref, salt_ref, land_ref, left_ref, right_ref, wleft_ref, wright_ref, prev_ref, next_ref,
    temp_out, salt_out, keep, gain, side, ubuf,
):
    level = pl.program_id(0)
    levels = pl.num_programs(0)
    tile_x = land_ref.shape[0]
    width = NSTEP
    chunk = 16
    lo = BASE - SUB
    span = tile_x + 2 * SUB
    spots = range(lo, lo + span, chunk)
    total = tile_x + 2 * BASE
    pieces = 2 * 8 + 1

    def extend(ref, centre, piece):
        ref[0:BASE] = jnp.zeros((BASE, LANES), F32)
        ref[BASE + tile_x : total] = jnp.zeros((BASE, LANES), F32)
        ref[BASE - width : BASE] = prev_ref[pl.ds(piece * width, width)]
        ref[BASE + tile_x : BASE + tile_x + width] = next_ref[pl.ds(piece * width, width)]
        ref[BASE : BASE + tile_x] = centre

    lane = iota((chunk, LANES), 1)
    pick = (lane & 7) == width

    @pl.when(level == 0)
    def _():
        extend(ubuf.at[0], land_ref[...].astype(F32), pieces - 1)
        names = ((left_ref, wleft_ref), (right_ref, wright_ref))
        for k, (strip, wstrip) in enumerate(names):
            extend(ubuf.at[1 + k], wstrip[...], pieces + 2 + k)
            extend(ubuf.at[3 + k], strip[...], pieces + k)
            for r in range(0, total, chunk):
                ubuf[3 + k, r : r + chunk] = ubuf[3 + k, r : r + chunk] * ubuf[1 + k, r : r + chunk]
        for r in spots:
            rows = pl.ds(r, chunk)
            wl = ubuf[1, rows]
            wr = ubuf[2, rows]
            wl_up = pltpu.roll(wl, 1, 1)
            wr_dn = pltpu.roll(wr, LANES - 1, 1)
            cross = pltpu.roll(jnp.where(pick, wl_up, wr_dn), LANES - width, 1)
            wet = ubuf[0, rows]
            west = jnp.where(lane == 0, cross, pltpu.roll(wet, 1, 1))
            east = jnp.where(lane == LANES - 1, cross, pltpu.roll(wet, LANES - 1, 1))
            near = west + east + ubuf[0, pl.ds(r - 1, chunk)] + ubuf[0, pl.ds(r + 1, chunk)]
            keep[0, rows] = 1.0 - KAPPA * wet * near
            gain[0, rows] = KAPPA * wet
            near = wl_up + pltpu.roll(wl, LANES - 1, 1)
            near = near + ubuf[1, pl.ds(r - 1, chunk)] + ubuf[1, pl.ds(r + 1, chunk)]
            keep[1, rows] = 1.0 - KAPPA * wl * near
            gain[1, rows] = KAPPA * wl
            near = wr_dn + pltpu.roll(wr, 1, 1)
            near = near + ubuf[2, pl.ds(r - 1, chunk)] + ubuf[2, pl.ds(r + 1, chunk)]
            keep[2, rows] = 1.0 - KAPPA * wr * near
            gain[2, rows] = KAPPA * wr
        for t in range(NSTEP):
            src = 3 if t % 2 == 0 else 1
            dst = 1 if t % 2 == 0 else 3
            for r in spots:
                rows = pl.ds(r, chunk)
                ul = ubuf[src, rows]
                ur = ubuf[src + 1, rows]
                ul_up = pltpu.roll(ul, 1, 1)
                ur_dn = pltpu.roll(ur, LANES - 1, 1)
                side[t, rows] = jnp.where(pick, ul_up, ur_dn)
                if t < NSTEP - 1:
                    near = ul_up + pltpu.roll(ul, LANES - 1, 1)
                    near = near + ubuf[src, pl.ds(r - 1, chunk)] + ubuf[src, pl.ds(r + 1, chunk)]
                    ubuf[dst, rows] = keep[1, rows] * ul + gain[1, rows] * near
                    near = ur_dn + pltpu.roll(ur, 1, 1)
                    near = near + ubuf[src + 1, pl.ds(r - 1, chunk)]
                    near = near + ubuf[src + 1, pl.ds(r + 1, chunk)]
                    ubuf[dst + 1, rows] = keep[2, rows] * ur + gain[2, rows] * near

    for k, (ref, out) in enumerate(((temp_ref, temp_out), (salt_ref, salt_out))):
        field = level + k * levels
        turn = rest(2 * LANES - 8 * field - width, LANES)
        a = 1 + 2 * k
        for pad, src in ((BASE - width, prev_ref), (BASE + tile_x, next_ref)):
            halo = src[pl.ds(field * width, width)]
            wet = src[pl.ds((pieces - 1) * width, width)]
            ubuf[a, pad : pad + width] = halo * wet
        for r in range(0, tile_x, chunk):
            ubuf[a, pl.ds(BASE + r, chunk)] = ref[0, r : r + chunk] * land_ref[r : r + chunk].astype(F32)
        for t in range(NSTEP):
            src = a + t % 2
            dst = a + 1 - t % 2
            for r in spots if t < NSTEP - 1 else range(BASE, BASE + tile_x, chunk):
                rows = pl.ds(r, chunk)
                u = ubuf[src, rows]
                cross = pltpu.roll(side[t, rows], turn, 1)
                west = jnp.where(lane == 0, cross, pltpu.roll(u, 1, 1))
                east = jnp.where(lane == LANES - 1, cross, pltpu.roll(u, LANES - 1, 1))
                near = west + east + ubuf[src, pl.ds(r - 1, chunk)] + ubuf[src, pl.ds(r + 1, chunk)]
                new = keep[0, rows] * u + gain[0, rows] * near
                if t < NSTEP - 1:
                    ubuf[dst, rows] = new
                else:
                    at = slice(r - BASE, r - BASE + chunk)
                    out[0, at] = jnp.where(land_ref[at] != 0, new, ref[0, at])


def share(level, levels, band):
    value = math.exp(-LEVEL_DEPTH * level / DEPTH_SCALE[band])
    if level < levels - 1:
        value = value - math.exp(-LEVEL_DEPTH * (level + 1) / DEPTH_SCALE[band])
    return value


def surface_kernel(
    cap, side, levels, tab_ref, in_ref, temp_ref, salt_ref, land_ref, east_ref, north_ref,
    force_ref, reply_ref, rows_in, rows_out,
):
    tile_x = land_ref.shape[0]
    blocks_x = tile_x // side
    blocks_y = LANES // side
    halves = side * side // LANES
    half = side // halves
    sent = 5 * halves
    back = 2 * halves
    devices = in_ref.shape[0]

    def band(bx, carry):
        for by in range(blocks_y):
            at = tab_ref[1, bx * blocks_y + by]
            pos = jnp.maximum(at, 0)
            value = in_ref[quot(pos, cap), pl.ds(rest(pos, cap) * sent, sent), :]
            held = jnp.full(value.shape, at, jnp.int32) >= 0
            rows_in[pl.ds(by, sent, stride=blocks_y), :] = jnp.where(held, value, 0.0)
        tile = swap_chunks(rows_in[...], side)
        replies = [None] * back
        for h in range(halves):
            rows = pl.ds(pl.multiple_of(bx * side + h * half, half), half)
            force = [tile[(f * halves + h) * half : (f * halves + h + 1) * half] for f in range(5)]
            for f in range(5):
                force_ref[f, rows] = force[f]
            wet = land_ref[rows].astype(F32)
            lit = force[3]
            for b in range(3):
                lit = lit + share(0, levels, b) * force[b]
            sst = temp_ref[0, rows] + 0.5 * wet * lit
            sss = salt_ref[0, rows] - 0.5 * wet * force[4]
            freezing = -0.3 * sss
            east = east_ref[rows]
            north = north_ref[rows]
            stress = jnp.sqrt(east * east + north * north + 1.0)
            replies[h] = -0.1 * stress * (sst - freezing)
            replies[halves + h] = freezing
        packed = swap_chunks(jnp.concatenate(replies, axis=0), side)
        rows_out[pl.ds(pl.multiple_of(bx * back * SUB, SUB), back * SUB), :] = packed
        return carry

    lax.fori_loop(0, blocks_x, band, 0)

    def answer(row, carry):
        for lane in range(LANES):
            local = tab_ref[2 + row, lane]
            start = quot(local, blocks_y) * (back * SUB) + rest(local, blocks_y)
            slot = row * LANES + lane
            reply_ref[quot(slot, cap), pl.ds(rest(lane, cap) * back, back), :] = rows_out[
                pl.ds(start, back, stride=SUB), :
            ]
        return carry

    lax.fori_loop(0, devices * cap // LANES, answer, 0)


def absorb_kernel(levels, temp_ref, salt_ref, force_ref, land_ref, temp_out, salt_out):
    half_wet = 0.5 * land_ref[...].astype(F32)
    force = [half_wet * force_ref[b] for b in range(3)]
    for level in range(levels):
        lit = share(level, levels, 0) * force[0]
        for b in range(1, 3):
            lit = lit + share(level, levels, b) * force[b]
        if level == 0:
            lit = lit + half_wet * force_ref[3]
            salt_out[level] = salt_ref[level] - half_wet * force_ref[4]
        else:
            salt_out[level] = salt_ref[level]
        temp_out[level] = temp_ref[level] + lit


def full(shape):
    return pl.BlockSpec(shape, lambda i: (0,) * len(shape))


def body(
    ice_blocks, ice_conc, ice_thick, ice_snow, ice_temp, sw_down,
    ocean_temp, ocean_salt, ocean_east, ocean_north, land_mask,
):
    n_grp = lax.axis_size("grp")
    n_gx = lax.axis_size("gx")
    n_gy = lax.axis_size("gy")
    devices = n_grp * n_gx * n_gy
    n_rows = n_grp * n_gy
    me = lax.axis_index(AXES).astype(jnp.int32).reshape(1)
    per_dev, cats, cells = ice_conc.shape
    layers = ice_temp.shape[2]
    side = math.isqrt(cells)
    halves = cells // LANES
    levels, tile_x, tile_y = ocean_temp.shape
    blocks_x = tile_x // side
    blocks_y = tile_y // side
    per_tile = blocks_x * blocks_y
    cap = 2 * max(1, per_tile // (2 * devices))
    slots = devices * cap
    sds = jax.ShapeDtypeStruct

    conc = ice_conc.transpose(1, 0, 2)
    thick = ice_thick.transpose(1, 0, 2)
    snow = ice_snow.transpose(1, 0, 2)
    sw = sw_down.transpose(1, 0, 2)
    temps = ice_temp.transpose(1, 2, 0, 3)

    tab = pl.pallas_call(
        functools.partial(
            table_kernel, (n_gx, n_gy, n_rows, blocks_x, blocks_y, per_dev, cap, devices)
        ),
        out_shape=sds((2 + slots // LANES, LANES), jnp.int32),
        in_specs=[SMEM, VMEM],
        out_specs=VMEM,
        name="tables",
    )(me, ice_blocks.reshape(-1, LANES))

    tile = sds((tile_x, LANES), F32)
    edge_rows = (2 * levels + 1) * NSTEP
    mix, wets, up, down, head, foot = pl.pallas_call(
        edge_kernel,
        out_shape=[tile] * 4 + [sds((edge_rows, LANES), F32)] * 2,
        in_specs=[VMEM] * 3,
        out_specs=[VMEM] * 6,
        name="edges",
    )(ocean_temp, ocean_salt, land_mask)
    rows_axis = ("grp", "gy")
    below = lax.ppermute(up, rows_axis, [(i, i + 1) for i in range(n_rows - 1)])
    above = lax.ppermute(down, rows_axis, [(i + 1, i) for i in range(n_rows - 1)])
    top = (n_grp - 1) * n_gx * n_gy + n_gy - 1
    fold = lax.ppermute(
        up, AXES, [(top + q * n_gy, top + (n_gx - 1 - q) * n_gy) for q in range(n_gx)]
    )

    chunk = per_dev // 4
    fields = 5 * halves
    outgoing = pl.pallas_call(
        functools.partial(optics_kernel, cap),
        out_shape=sds((devices, cap * fields, LANES), F32),
        grid=(per_dev // chunk,),
        in_specs=[SMEM]
        + [pl.BlockSpec((cats, chunk, cells), lambda i: (0, i, 0))] * 3
        + [
            pl.BlockSpec((3, chunk, cells), lambda i: (0, i, 0)),
            pl.BlockSpec((cats, 1, chunk, cells), lambda i: (0, layers - 1, i, 0)),
        ],
        out_specs=full((devices, cap * fields, LANES)),
        scratch_shapes=[pltpu.VMEM((fields * chunk, LANES), F32)],
        name="optics",
    )(tab, conc, thick, snow, sw, temps)
    incoming = lax.all_to_all(outgoing, AXES, split_axis=0, concat_axis=0, tiled=True)

    all_rows = edge_rows + 4 * NSTEP
    left, right, wleft, wright, first, last = pl.pallas_call(
        functools.partial(strip_kernel, (n_grp, n_gx, n_gy)),
        out_shape=[tile] * 4 + [sds((all_rows, LANES), F32)] * 2,
        in_specs=[SMEM] + [VMEM] * 7,
        out_specs=[VMEM] * 6,
        name="strips",
    )(me, mix, wets, above, below, fold, head, foot)
    before = lax.ppermute(last, "gx", [(i, (i + 1) % n_gx) for i in range(n_gx)])
    after = lax.ppermute(first, "gx", [((i + 1) % n_gx, i) for i in range(n_gx)])

    level_spec = pl.BlockSpec((1, tile_x, tile_y), lambda i: (i, 0, 0))
    ext = (tile_x + 2 * BASE, LANES)
    temp_mid, salt_mid = pl.pallas_call(
        diffuse_kernel,
        out_shape=[sds(ocean_temp.shape, F32)] * 2,
        grid=(levels,),
        in_specs=[level_spec] * 2 + [full((tile_x, LANES))] * 5 + [full((all_rows, LANES))] * 2,
        out_specs=[level_spec] * 2,
        scratch_shapes=[
            pltpu.VMEM((3,) + ext, F32),
            pltpu.VMEM((3,) + ext, F32),
            pltpu.VMEM((NSTEP,) + ext, F32),
            pltpu.VMEM((5,) + ext, F32),
        ],
        name="diffuse",
    )(ocean_temp, ocean_salt, land_mask, left, right, wleft, wright, before, after)

    back = 2 * halves
    force, reply = pl.pallas_call(
        functools.partial(surface_kernel, cap, side, levels),
        out_shape=[
            sds((5, tile_x, tile_y), F32),
            sds((devices, cap * back, LANES), F32),
        ],
        grid=(1,),
        in_specs=[SMEM, full(incoming.shape)]
        + [pl.BlockSpec((1, tile_x, tile_y), lambda i: (0, 0, 0))] * 2
        + [full((tile_x, tile_y))] * 3,
        out_specs=[full((5, tile_x, tile_y)), full((devices, cap * back, LANES))],
        scratch_shapes=[
            pltpu.VMEM((fields * SUB, LANES), F32),
            pltpu.VMEM((blocks_x * back * SUB, LANES), F32),
        ],
        name="surface",
    )(tab, incoming, temp_mid, salt_mid, land_mask, ocean_east, ocean_north)
    answered = lax.all_to_all(reply, AXES, split_axis=0, concat_axis=0, tiled=True)

    temp_new, salt_new = pl.pallas_call(
        functools.partial(absorb_kernel, levels),
        out_shape=[sds(ocean_temp.shape, F32)] * 2,
        in_specs=[VMEM] * 4,
        out_specs=[VMEM] * 2,
        name="absorb",
    )(temp_mid, salt_mid, force, land_mask)

    cat_spec = pl.BlockSpec((1, per_dev, cells), lambda i: (i, 0, 0))
    warm = pl.pallas_call(
        warm_kernel,
        out_shape=sds(temps.shape, F32),
        grid=(cats,),
        in_specs=[
            cat_spec,
            cat_spec,
            full((3, per_dev, cells)),
            pl.BlockSpec((1, layers, per_dev, cells), lambda i: (i, 0, 0, 0)),
        ],
        out_specs=pl.BlockSpec((1, layers, per_dev, cells), lambda i: (i, 0, 0, 0)),
        name="warm",
    )(thick, snow, sw, temps)

    bottom = pl.BlockSpec((cats, 1, per_dev, cells), lambda i: (0, layers - 1, 0, 0))
    thick_new, temps_new = pl.pallas_call(
        functools.partial(finish_kernel, cap),
        out_shape=[sds(thick.shape, F32), sds(temps.shape, F32)],
        grid=(1,),
        in_specs=[SMEM, full(answered.shape), full(thick.shape), bottom],
        out_specs=[full(thick.shape), bottom],
        scratch_shapes=[pltpu.VMEM((back * per_dev, LANES), F32)],
        input_output_aliases={3: 1},
        name="finish",
    )(tab, answered, thick, warm)
    return (
        temps_new.transpose(2, 0, 1, 3),
        thick_new.transpose(1, 0, 2),
        temp_new,
        salt_new,
    )


def solution(mesh):
    placed = (
        P(),
        P(AXES, None, None),
        P(AXES, None, None),
        P(AXES, None, None),
        P(AXES, None, None, None),
        P(AXES, None, None),
        P(None, "gx", ("grp", "gy")),
        P(None, "gx", ("grp", "gy")),
        P("gx", ("grp", "gy")),
        P("gx", ("grp", "gy")),
        P("gx", ("grp", "gy")),
    )
    return jax.shard_map(
        body,
        mesh=mesh,
        in_specs=placed,
        out_specs=(
            P(AXES, None, None, None),
            P(AXES, None, None),
            P(None, "gx", ("grp", "gy")),
            P(None, "gx", ("grp", "gy")),
        ),
        check_vma=False,
    )
```
